256 devices in a mesh: shot: 16 (over z_hi, y, core), dom: 16 (over x, z_lo).
Axes of the slice: x: 4, y: 4, z: 8 (z_hi: 2, z_lo: 4; z = z_hi * 4 + z_lo), core: 2. Of those that a mesh axis runs over, the one named last changes fastest.
Arguments:
- model_slab: float32 [256, 128, 128], P('dom'), may hold values from 0.0225 to 0.17
- wave_prev: float32 [16, 256, 128, 128], P('shot', 'dom'), may hold values from -6 to 6
- wave_now: float32 [16, 256, 128, 128], P('shot', 'dom'), may hold values from -6 to 6
- adjoint_next: float32 [16, 256, 128, 128], P('shot', 'dom'), may hold values from -6 to 6
- adjoint_now: float32 [16, 256, 128, 128], P('shot', 'dom'), may hold values from -6 to 6
- wavelet: float32 [16, 8], P('shot'), may hold values from -12 to 12
- source_cell: int32 [16], P('shot'), may hold values from 0 to 4194303
- receiver_cells: int32 [16, 256], P('shot'), may hold values from 0 to 4194303
- observed: float32 [16, 8, 256], P('shot'), may hold values from -6 to 6
Outputs:
- direction: float32 [256, 128, 128], P('dom')
- new_model: float32 [256, 128, 128], P('dom')
The draws below stay inside these ranges and needn't reach their ends.
Inputs may be any that keep to these rules, and one draw needn't show every extreme that they name: `source_cell`: flat cell index x * 128 * 128 + y * 128 + z. `receiver_cells`: flat cell indices x * 128 * 128 + y * 128 + z; a cell may repeat.
All inputs are finite; a program needn't handle non-finite values. Where the reference program divides by a largest or mean magnitude, that divisor is 1e-20 or more.
Results may differ from the reference program's by a relative error of at most 0.000025.
Values sent between devices are 32-bit elements; how exact they have to be, the bound alone decides.
No kernel may reach another device: no remote copies, remote signals or barrier semaphores. Data moves between devices by JAX's collectives and lax.ppermute only.
A program may use at most 192 MiB of HBM per device.

```python
import math
import jax
import jax.numpy as jnp
from jax import lax

NY = 128
NZ = 128
STEPS = 8
REC = 256
NX = 256
SHOTS = 16


def plant(array, rng, smallest, top_value):
    longest = array.shape.index(max(array.shape))
    spots = []
    for shift in (0, 1):
        where = [jax.random.randint(jax.random.fold_in(rng, axis), (), 0, length) for axis, length in enumerate(array.shape)]
        where[longest] = (where[longest] + shift) % array.shape[longest]
        spots.append(tuple(where))
    return array.at[spots[0]].set(smallest).at[spots[1]].set(top_value)


def levels(key, extent, cuts, least, largest):
    def one(axis_at, blocks):
        heights = jax.random.uniform(jax.random.fold_in(jax.random.fold_in(key, 6), axis_at), (blocks,), jnp.float32, least / len(cuts), largest / len(cuts))
        return jnp.repeat(jnp.exp(heights), extent[axis_at] // blocks).reshape((-1,) + (1,) * (len(extent) - axis_at - 1))

    loudness = one(*cuts[0])
    for cut in cuts[1:]:
        loudness = loudness * one(*cut)
    return loudness


def scatter_about(rng, extent, deviation, bound, split=(), kind=jnp.bfloat16):
    result = deviation * jax.random.normal(rng, extent, jnp.float32)
    if split:
        result = result * levels(rng, extent, split, -0.22, 0.18)
    return jnp.clip(result, -bound, bound).astype(kind)


def setup_inputs(seed: int = 0) -> dict:
    streams_of = jax.random.split(jax.random.key(seed), 10)
    return {
        "model_slab": jnp.clip(jnp.exp(math.log(0.17) - 2.022283 * jax.random.uniform(streams_of[0], (NX, NY, NZ), jnp.float32) ** levels(streams_of[0], (NX, NY, NZ), ((0, 16),), -0.2, 0.2)), 0.0225, 0.17),
        "wave_prev": scatter_about(streams_of[1], (SHOTS, NX, NY, NZ), 1.0, 6.0, ((0, 16), (1, 16)), jnp.float32),
        "wave_now": scatter_about(streams_of[2], (SHOTS, NX, NY, NZ), 1.0, 6.0, ((0, 16), (1, 16)), jnp.float32),
        "adjoint_next": scatter_about(streams_of[3], (SHOTS, NX, NY, NZ), 1.0, 6.0, ((0, 16), (1, 16)), jnp.float32),
        "adjoint_now": scatter_about(streams_of[4], (SHOTS, NX, NY, NZ), 1.0, 6.0, ((0, 16), (1, 16)), jnp.float32),
        "wavelet": scatter_about(streams_of[5], (SHOTS, STEPS), 3.0, 12.0, ((0, 16),), jnp.float32),
        "source_cell": plant(jax.random.randint(streams_of[6], (SHOTS,), 0, NX * NY * NZ), jax.random.fold_in(streams_of[6], 1), 0, (NX * NY * NZ) - 1).astype(jnp.int32),
        "receiver_cells": plant(jax.random.randint(streams_of[7], (SHOTS, REC), 0, NX * NY * NZ), jax.random.fold_in(streams_of[7], 1), 0, (NX * NY * NZ) - 1).astype(jnp.int32),
        "observed": scatter_about(streams_of[8], (SHOTS, STEPS, REC), 1.0, 6.0, ((0, 16),), jnp.float32),
    }


COEFFS = (8.0 / 5.0, -1.0 / 5.0, 8.0 / 315.0, -1.0 / 560.0)
CENTRE = -205.0 / 72.0
STEP_FRACTION = 0.1
EPSILON = 1e-6


def shifted(field, axis, offset):
    length = field.shape[axis]
    filler_shape = list(field.shape)
    filler_shape[axis] = abs(offset)
    filler = jnp.zeros(filler_shape, field.dtype)
    if offset > 0:
        return jnp.concatenate([lax.slice_in_dim(field, offset, length, axis=axis), filler], axis)
    return jnp.concatenate([filler, lax.slice_in_dim(field, 0, length + offset, axis=axis)], axis)


def laplace(field):
    total = (3.0 * CENTRE) * field
    for axis in (0, 1, 2):
        for index, weight in enumerate(COEFFS):
            offset = index + 1
            total = total + weight * (shifted(field, axis, offset) + shifted(field, axis, -offset))
    return total


def one_shot(model_slab, wave_prev, wave_now, adjoint_next, adjoint_now, wavelet_row, source_one, receivers, observed_rows):
    shape = wave_now.shape
    images = []
    residuals = []
    older, current = wave_prev, wave_now
    for tick in range(STEPS):
        image = laplace(current)
        newer = 2.0 * current - older + model_slab * image
        newer = newer.reshape(-1).at[source_one].add(wavelet_row[tick]).reshape(shape)
        residuals.append(newer.reshape(-1)[receivers] - observed_rows[tick])
        images.append(image)
        older, current = current, newer
    later, present = adjoint_next, adjoint_now
    gradient = jnp.zeros(shape, jnp.float32)
    for tick in reversed(range(STEPS)):
        earlier = 2.0 * present - later + model_slab * laplace(present)
        earlier = earlier.reshape(-1).at[receivers].add(residuals[tick]).reshape(shape)
        gradient = gradient + earlier * images[tick]
        later, present = present, earlier
    return gradient


def reference(model_slab, wave_prev, wave_now, adjoint_next, adjoint_now, wavelet, source_cell, receiver_cells, observed):
    def accumulate(total, items):
        return total + one_shot(model_slab, *items), None

    start = jnp.zeros(model_slab.shape, jnp.float32)
    total, unused = lax.scan(accumulate, start, (wave_prev, wave_now, adjoint_next, adjoint_now, wavelet, source_cell, receiver_cells, observed))
    peak = jnp.max(jnp.abs(total))
    direction = total / (peak + EPSILON)
    new_model = model_slab * (1.0 - STEP_FRACTION * direction)
    return direction, new_model
```

```python
import functools
import jax
import jax.numpy as jnp
from jax import lax
from jax.experimental import pallas as pl
from jax.experimental.pallas import tpu as pltpu
from jax.sharding import PartitionSpec as P

STEPS = 8
COEFFS = (8.0 / 5.0, -1.0 / 5.0, 8.0 / 315.0, -1.0 / 560.0)
CENTRE = -205.0 / 72.0
STEP_FRACTION = 0.1
EPSILON = 1e-06
ROWS = 16
NY = 128
NZ = 128
REC = 256
EDGE = 4
MID = ROWS - 2 * EDGE
CHUNK = 32
VMEM = pl.BlockSpec(memory_space=pltpu.VMEM)
SMEM = pl.BlockSpec(memory_space=pltpu.SMEM)
LIMIT = 24 * 1024 * 1024


def planes(count):
    return jax.ShapeDtypeStruct((count, NY, NZ), jnp.float32)


def call(kernel, outs, scratch, specs, out_specs, flops, nbytes, name, aliases={}):
    return pl.pallas_call(
        kernel,
        out_shape=outs,
        in_specs=specs,
        out_specs=out_specs,
        scratch_shapes=scratch,
        input_output_aliases=aliases,
        compiler_params=pltpu.CompilerParams(vmem_limit_bytes=LIMIT),
        cost_estimate=pl.CostEstimate(flops=flops, transcendentals=0, bytes_accessed=nbytes),
        name=name,
    )


def sort_kernel(first_ref, receivers_ref, lists_ref):
    for region in range(3):
        lists_ref[region, REC] = 0

    def body(j, carry):
        plane = (receivers_ref[0, j] - first_ref[0]) >> 14
        inside = (plane >= 0) & (plane < ROWS)
        region = jnp.where(plane < EDGE, 0, jnp.where(plane < ROWS - EDGE, 1, 2))

        @pl.when(inside)
        def _():
            count = lists_ref[region, REC]
            lists_ref[region, count] = j
            lists_ref[region, REC] = count + 1

        return carry

    lax.fori_loop(0, REC, body, 0)


def where_of(cell, first):
    local = cell - first
    return local >> 14, (local >> 7) & 127, local & 127


def lanes_row():
    return lax.broadcasted_iota(jnp.int32, (1, NZ), 1)


def add_source(first_ref, source_ref, wavelet_ref, tick, ref, low, count):
    plane, row, lane = where_of(source_ref[0], first_ref[0])
    plane = plane - low

    @pl.when((plane >= 0) & (plane < count))
    def _():
        extra = jnp.where(lanes_row() == lane, wavelet_ref[0, tick], 0.0)
        spot = ref[plane, pl.ds(row, 1), :]
        ref[plane, pl.ds(row, 1), :] = spot + extra


def add_residuals(first_ref, receivers_ref, lists_ref, res_ref, ref, region, low):
    def body(i, carry):
        j = lists_ref[region, i]
        plane, row, lane = where_of(receivers_ref[0, j], first_ref[0])
        spot = ref[plane - low, pl.ds(row, 1), :]
        ref[plane - low, pl.ds(row, 1), :] = spot + res_ref[pl.ds(j, 1), :]
        return carry

    lax.fori_loop(0, lists_ref[region, REC], body, 0)


def take_residuals(first_ref, receivers_ref, lists_ref, observed_ref, tick, refs, res_ref):
    lows = (0, EDGE, ROWS - EDGE)
    for region in range(3):
        ref, low = refs[region], lows[region]

        def body(i, carry):
            j = lists_ref[region, i]
            plane, row, lane = where_of(receivers_ref[0, j], first_ref[0])
            spot = ref[plane - low, pl.ds(row, 1), :]
            value = spot - observed_ref[tick, j]
            res_ref[pl.ds(j, 1), :] = jnp.where(lanes_row() == lane, value, 0.0)
            return carry

        lax.fori_loop(0, lists_ref[region, REC], body, 0)


def fill_padded(pad_ref, lo_ref, mid_ref, hi_ref):
    zeros = jnp.zeros((8, NZ), jnp.float32)
    for i in range(EDGE):
        pad_ref[i] = jnp.zeros((NY + 16, NZ), jnp.float32)
        pad_ref[ROWS + EDGE + i] = jnp.zeros((NY + 16, NZ), jnp.float32)
    start = EDGE
    for ref, count in ((lo_ref, EDGE), (mid_ref, MID), (hi_ref, EDGE)):

        def body(i, carry, ref=ref, start=start):
            pad_ref[start + i, pl.ds(0, 8), :] = zeros
            pad_ref[start + i, pl.ds(NY + 8, 8), :] = zeros
            pad_ref[start + i, pl.ds(8, NY), :] = ref[i]
            return carry

        lax.fori_loop(0, count, body, 0)
        start += count


def laplace_rows(pad_ref, plane, row, lane_weights):
    at = plane + EDGE
    field = pad_ref[at, pl.ds(8 + row, CHUNK), :]
    total = (3.0 * CENTRE) * field
    for index, weight in enumerate(COEFFS):
        k = index + 1
        pair = pad_ref[at + k, pl.ds(8 + row, CHUNK), :] + pad_ref[at - k, pl.ds(8 + row, CHUNK), :]
        pair = pair + (pad_ref[at, pl.ds(8 + row + k, CHUNK), :] + pad_ref[at, pl.ds(8 + row - k, CHUNK), :])
        total = total + weight * pair
        total = total + lane_weights[2 * index] * pltpu.roll(field, NZ - k, 1)
        total = total + lane_weights[2 * index + 1] * pltpu.roll(field, k, 1)
    return field, total


def make_lane_weights():
    lane = lax.broadcasted_iota(jnp.int32, (CHUNK, NZ), 1)
    out = []
    for index, weight in enumerate(COEFFS):
        k = index + 1
        out.append(jnp.where(lane < NZ - k, weight, 0.0))
        out.append(jnp.where(lane >= k, weight, 0.0))
    return out


def own_kernel(forward, tick, has_extra, *refs):
    refs = list(refs)
    take = lambda n: [refs.pop(0) for _ in range(n)]
    first_ref, receivers_ref, lists_ref = take(3)
    if forward:
        source_ref, wavelet_ref = take(2)
    observed = take(1)[0] if (forward and tick > 0) or (not forward and tick == STEPS - 1) else None
    cur = take(3)
    old = take(3)
    model = take(3)
    if not forward:
        if tick == STEPS - 1:
            last = take(3)
        else:
            res_in = take(1)[0]
        if has_extra:
            image = take(3)
            grad_in = take(1)[0]
    next_mid, base_lo, base_hi = take(3)
    if forward:
        image_out = take(3)
        res_out = take(1)[0] if tick > 0 else None
    else:
        res_out = take(1)[0] if tick == STEPS - 1 else None
        grad_out = take(1)[0] if has_extra or tick == STEPS - 1 else None
    pad_ref = take(1)[0]

    fill_padded(pad_ref, *cur)
    weights = make_lane_weights()
    outs = (base_lo, next_mid, base_hi)
    low = 0
    for region, count in enumerate((EDGE, MID, EDGE)):

        def body(i, carry, region=region, low=low):
            for row in range(0, NY, CHUNK):
                field, total = laplace_rows(pad_ref, low + i, row, weights)
                rows = pl.ds(row, CHUNK)
                value = 2.0 * field - old[region][i, rows, :] + model[region][i, rows, :] * total
                outs[region][i, rows, :] = value
                if forward:
                    image_out[region][i, rows, :] = total
                elif has_extra:
                    grad_out[low + i, rows, :] = grad_in[low + i, rows, :] + field * image[region][i, rows, :]
                elif grad_out is not None:
                    grad_out[low + i, rows, :] = jnp.zeros((CHUNK, NZ), jnp.float32)
            return carry

        lax.fori_loop(0, count, body, 0)
        low += count

    if forward:
        add_source(first_ref, source_ref, wavelet_ref, tick, next_mid, EDGE, MID)
        if tick > 0:
            take_residuals(first_ref, receivers_ref, lists_ref, observed, tick - 1, cur, res_out)
    else:
        if tick == STEPS - 1:
            take_residuals(first_ref, receivers_ref, lists_ref, observed, tick, last, res_out)
            res_in = res_out
        add_residuals(first_ref, receivers_ref, lists_ref, res_in, next_mid, 1, EDGE)


def edge_kernel(forward, tick, *refs):
    refs = list(refs)
    take = lambda n: [refs.pop(0) for _ in range(n)]
    first_ref, receivers_ref, lists_ref = take(3)
    if forward:
        source_ref, wavelet_ref = take(2)
    before, after, base_lo, base_hi, model_lo, model_hi = take(6)
    if forward:
        part_lo, part_hi = take(2)
    else:
        res_ref = take(1)[0]
    next_lo, next_hi = take(2)
    if forward:
        image_lo, image_hi = take(2)

    def body(c, carry):
        rows = pl.ds(pl.multiple_of(c * CHUNK, CHUNK), CHUNK)
        low = [before[i, rows, :] for i in range(EDGE)]
        high = [after[i, rows, :] for i in range(EDGE)]
        for j in range(EDGE):
            extra = COEFFS[3] * low[j]
            for k in range(j + 1, 4):
                extra = extra + COEFFS[k - 1] * low[EDGE + j - k]
            next_lo[j, rows, :] = base_lo[j, rows, :] + model_lo[j, rows, :] * extra
            if forward:
                image_lo[j, rows, :] = part_lo[j, rows, :] + extra
            extra = COEFFS[3] * high[j]
            for k in range(EDGE - j, 4):
                extra = extra + COEFFS[k - 1] * high[j + k - EDGE]
            next_hi[j, rows, :] = base_hi[j, rows, :] + model_hi[j, rows, :] * extra
            if forward:
                image_hi[j, rows, :] = part_hi[j, rows, :] + extra
        return carry

    lax.fori_loop(0, NY // CHUNK, body, 0)
    if forward:
        add_source(first_ref, source_ref, wavelet_ref, tick, next_lo, 0, EDGE)
        add_source(first_ref, source_ref, wavelet_ref, tick, next_hi, ROWS - EDGE, EDGE)
    else:
        add_residuals(first_ref, receivers_ref, lists_ref, res_ref, next_lo, 0, 0)
        add_residuals(first_ref, receivers_ref, lists_ref, res_ref, next_hi, 2, ROWS - EDGE)


def swap(value, axis, pairs):
    return lax.ppermute(value, axis, pairs)


def shot_sum(grad):
    shot = lax.axis_index("shot")
    core = shot % 2
    y = (shot // 2) % 4
    other_core = [(k, k ^ 1) for k in range(16)]
    other_z = [(k, k ^ 8) for k in range(16)]

    def turn(r):
        return [(k, (k // 8) * 8 + ((k // 2 + r) % 4) * 2 + k % 2) for k in range(16)]

    keep = lax.dynamic_slice_in_dim(grad, core * 8, 8, 0)
    send = lax.dynamic_slice_in_dim(grad, (1 - core) * 8, 8, 0)
    half = keep + swap(send, "shot", other_core)
    parts = [lax.dynamic_slice_in_dim(half, ((y + r) % 4) * 2, 2, 0) for r in range(4)]
    got = [swap(parts[r], "shot", turn(r)) for r in (1, 2, 3)]
    part = parts[0] + got[0] + got[1] + got[2]
    part = part + swap(part, "shot", other_z)
    got = [part] + [swap(part, "shot", turn(r)) for r in (1, 2, 3)]
    half = jnp.zeros((8, NY, NZ), jnp.float32)
    for r in range(4):
        half = lax.dynamic_update_slice_in_dim(half, got[r], ((y - r) % 4) * 2, 0)
    other = swap(half, "shot", other_core)
    first = jnp.where(core == 0, half, other)
    second = jnp.where(core == 0, other, half)
    return jnp.concatenate([first, second])


def dom_max(value):
    value = jnp.broadcast_to(value, (8, 128))

    def along_x(r):
        return [(k, ((k // 4 + r) % 4) * 4 + k % 4) for k in range(16)]

    def along_z(r):
        return [(k, (k // 4) * 4 + (k + r) % 4) for k in range(16)]

    for turn in (along_x, along_z):
        got = [swap(value, "dom", turn(r)) for r in (1, 2, 3)]
        value = jnp.maximum(jnp.maximum(value, got[0]), jnp.maximum(got[1], got[2]))
    return value[0, 0]


def on_device(model_slab, wave_prev, wave_now, adjoint_next, adjoint_now, wavelet, source_cell, receiver_cells, observed):
    cut = lambda a: (a[:EDGE], a[EDGE : ROWS - EDGE], a[ROWS - EDGE :])
    up = [(i, i + 1) for i in range(15)]
    down = [(i + 1, i) for i in range(15)]
    first = (lax.axis_index("dom") * (ROWS * NY * NZ)).astype(jnp.int32).reshape(1)
    lists = call(
        sort_kernel,
        jax.ShapeDtypeStruct((3, REC + 128), jnp.int32),
        [],
        [SMEM, SMEM],
        SMEM,
        1000,
        4096,
        "sort_receivers",
    )(first, receiver_cells)
    observed = observed[0]
    where = (first, receiver_cells, lists)
    model = cut(model_slab)
    pad = [pltpu.VMEM((ROWS + 2 * EDGE, NY + 16, NZ), jnp.float32)]
    res_shape = jax.ShapeDtypeStruct((REC, NZ), jnp.float32)
    own_cost = dict(flops=ROWS * NY * NZ * 60, nbytes=8 * ROWS * NY * NZ * 4)
    edge_cost = dict(flops=2 * EDGE * NY * NZ * 10, nbytes=6 * EDGE * NY * NZ * 4)

    def halos(cur):
        return swap(cur[2], "dom", up), swap(cur[0], "dom", down)

    old, cur = cut(wave_prev[0]), cut(wave_now[0])
    images, residuals = [], []
    for tick in range(STEPS):
        before, after = halos(cur)
        extra = (observed,) if tick > 0 else ()
        outs = [planes(MID), planes(EDGE), planes(EDGE), planes(EDGE), planes(MID), planes(EDGE)]
        outs += [res_shape] if tick > 0 else []
        result = call(
            functools.partial(own_kernel, True, tick, False),
            outs,
            pad,
            [SMEM] * (5 + len(extra)) + [VMEM] * 9,
            [VMEM] * len(outs),
            name="own_forward",
            **own_cost,
        )(*where, source_cell, wavelet, *extra, *cur, *old, *model)
        mid, base_lo, base_hi, part_lo, image_mid, part_hi = result[:6]
        if tick > 0:
            residuals.append(result[6])
        low, high, image_lo, image_hi = call(
            functools.partial(edge_kernel, True, tick),
            [planes(EDGE)] * 4,
            [],
            [SMEM] * 5 + [VMEM] * 8,
            [VMEM] * 4,
            name="edge_forward",
            **edge_cost,
        )(*where, source_cell, wavelet, before, after, base_lo, base_hi, model[0], model[2], part_lo, part_hi)
        images.append((image_lo, image_mid, image_hi))
        old, cur = cur, (low, mid, high)
    last = cur
    old, cur = cut(adjoint_next[0]), cut(adjoint_now[0])
    grad = None
    for tick in reversed(range(STEPS)):
        before, after = halos(cur)
        top = tick == STEPS - 1
        extra = (observed,) if top else ()
        fields = last if top else (residuals[tick], *images[tick + 1], grad)
        outs = [planes(MID), planes(EDGE), planes(EDGE)]
        outs += [res_shape] if top else []
        outs += [planes(ROWS)]
        result = call(
            functools.partial(own_kernel, False, tick, not top),
            outs,
            pad,
            [SMEM] * (3 + len(extra)) + [VMEM] * (9 + len(fields)),
            [VMEM] * len(outs),
            name="own_adjoint",
            **own_cost,
        )(*where, *extra, *cur, *old, *model, *fields)
        mid, base_lo, base_hi = result[:3]
        if top:
            residuals.append(result[3])
        grad = result[-1]
        low, high = call(
            functools.partial(edge_kernel, False, tick),
            [planes(EDGE)] * 2,
            [],
            [SMEM] * 3 + [VMEM] * 7,
            [VMEM] * 2,
            name="edge_adjoint",
            **edge_cost,
        )(*where, before, after, base_lo, base_hi, model[0], model[2], residuals[tick])
        old, cur = cur, (low, mid, high)
    grad = grad + jnp.concatenate([a * b for a, b in zip(cur, images[0])])
    total = shot_sum(grad)
    peak = dom_max(jnp.max(jnp.abs(total)))
    direction = total / (peak + EPSILON)
    new_model = model_slab * (1.0 - STEP_FRACTION * direction)
    return direction, new_model


def solution(mesh):
    placed = (
        P("dom", None, None),
        P("shot", "dom", None, None),
        P("shot", "dom", None, None),
        P("shot", "dom", None, None),
        P("shot", "dom", None, None),
        P("shot", None),
        P("shot"),
        P("shot", None),
        P("shot", None, None),
    )
    return jax.shard_map(
        on_device,
        mesh=mesh,
        in_specs=placed,
        out_specs=(P("dom", None, None), P("dom", None, None)),
        check_vma=False,
    )
```

```python
import functools
import jax
import jax.numpy as jnp
from jax import lax
from jax.experimental import pallas as pl
from jax.experimental.pallas import tpu as pltpu
from jax.sharding import PartitionSpec as P

STEPS = 8
COEFFS = (8.0 / 5.0, -1.0 / 5.0, 8.0 / 315.0, -1.0 / 560.0)
CENTRE = -205.0 / 72.0
STEP_FRACTION = 0.1
EPSILON = 1e-06
ROWS = 16
NY = 128
NZ = 128
REC = 256
EDGE = 4
MID = ROWS - 2 * EDGE
CHUNK = 32
SLICE = 8
VMEM = pl.BlockSpec(memory_space=pltpu.VMEM)
SMEM = pl.BlockSpec(memory_space=pltpu.SMEM)
LIMIT = 12 * 1024 * 1024


def planes(count):
    return jax.ShapeDtypeStruct((count, NY, NZ), jnp.float32)


def call(kernel, outs, scratch, specs, out_specs, flops, nbytes, name, aliases={}):
    return pl.pallas_call(
        kernel,
        out_shape=outs,
        in_specs=specs,
        out_specs=out_specs,
        scratch_shapes=scratch,
        input_output_aliases=aliases,
        compiler_params=pltpu.CompilerParams(vmem_limit_bytes=LIMIT),
        cost_estimate=pl.CostEstimate(flops=flops, transcendentals=0, bytes_accessed=nbytes),
        name=name,
    )


def sort_kernel(first_ref, receivers_ref, lists_ref):
    def body(j, counts):
        plane = where_of(receivers_ref[0, j], first_ref)[0]
        inside = (plane >= 0) & (plane < ROWS)
        low = inside & (plane < EDGE)
        high = inside & (plane >= ROWS - EDGE)
        mid = inside & (plane >= EDGE) & (plane < ROWS - EDGE)
        lists_ref[jnp.where(low, 0, 3), counts[0]] = j
        lists_ref[jnp.where(mid, 1, 3), counts[1]] = j
        lists_ref[jnp.where(high, 2, 3), counts[2]] = j
        return tuple(c + x.astype(jnp.int32) for c, x in zip(counts, (low, mid, high)))

    zero = jnp.int32(0)
    counts = lax.fori_loop(0, REC, body, (zero, zero, zero), unroll=4)
    for region in range(3):
        lists_ref[region, REC] = counts[region]


def where_of(cell, first_ref):
    local = cell - first_ref[0]
    plane = local >> 14
    plane = jnp.where(first_ref[1] == 1, ROWS - 1 - plane, plane)
    return plane, (local >> 7) & 127, local & 127


def cut_kernel(first_ref, whole_ref, low_ref, mid_ref, high_ref):
    start = 0
    for ref, count in ((low_ref, EDGE), (mid_ref, MID), (high_ref, EDGE)):

        def body(i, carry, ref=ref, start=start):
            plane = jnp.where(first_ref[1] == 1, ROWS - 1 - start - i, start + i)
            ref[i] = whole_ref[plane]
            return carry

        lax.fori_loop(0, count, body, 0)
        start += count


def join_kernel(first_ref, grad_ref, a_low, a_mid, a_high, b_low, b_mid, b_high, out_ref):
    start = 0
    for a, b, count in ((a_low, b_low, EDGE), (a_mid, b_mid, MID), (a_high, b_high, EDGE)):

        def body(i, carry, a=a, b=b, start=start):
            plane = jnp.where(first_ref[1] == 1, ROWS - 1 - start - i, start + i)
            out_ref[plane] = grad_ref[start + i] + a[i] * b[i]
            return carry

        lax.fori_loop(0, count, body, 0)
        start += count


def lanes_row():
    return lax.broadcasted_iota(jnp.int32, (1, NZ), 1)


def add_source(first_ref, source_ref, wavelet_ref, tick, ref, low, count):
    plane, row, lane = where_of(source_ref[0], first_ref)
    plane = plane - low

    @pl.when((plane >= 0) & (plane < count))
    def _():
        extra = jnp.where(lanes_row() == lane, wavelet_ref[0, tick], 0.0)
        spot = ref[plane, pl.ds(row, 1), :]
        ref[plane, pl.ds(row, 1), :] = spot + extra


def add_residuals(first_ref, receivers_ref, lists_ref, res_ref, ref, region, low):
    def body(i, carry):
        j = lists_ref[region, i]
        plane, row, lane = where_of(receivers_ref[0, j], first_ref)
        spot = ref[plane - low, pl.ds(row, 1), :]
        ref[plane - low, pl.ds(row, 1), :] = spot + res_ref[pl.ds(j, 1), :]
        return carry

    lax.fori_loop(0, lists_ref[region, REC], body, 0)


def take_residuals(first_ref, receivers_ref, lists_ref, observed_ref, tick, refs, res_ref):
    lows = (0, EDGE, ROWS - EDGE)
    for region in range(3):
        ref, low = refs[region], lows[region]

        def body(i, carry):
            j = lists_ref[region, i]
            plane, row, lane = where_of(receivers_ref[0, j], first_ref)
            spot = ref[plane - low, pl.ds(row, 1), :]
            value = spot - observed_ref[tick, j]
            res_ref[pl.ds(j, 1), :] = jnp.where(lanes_row() == lane, value, 0.0)
            return carry

        lax.fori_loop(0, lists_ref[region, REC], body, 0)


def fill_padded(pad_ref, lo_ref, mid_ref, hi_ref):
    zeros = jnp.zeros((8, NZ), jnp.float32)
    for i in range(EDGE):
        pad_ref[i] = jnp.zeros((NY + 16, NZ), jnp.float32)
        pad_ref[ROWS + EDGE + i] = jnp.zeros((NY + 16, NZ), jnp.float32)
    start = EDGE
    for ref, count in ((lo_ref, EDGE), (mid_ref, MID), (hi_ref, EDGE)):

        def body(i, carry, ref=ref, start=start):
            pad_ref[start + i, pl.ds(0, 8), :] = zeros
            pad_ref[start + i, pl.ds(NY + 8, 8), :] = zeros
            pad_ref[start + i, pl.ds(8, NY), :] = ref[i]
            return carry

        lax.fori_loop(0, count, body, 0)
        start += count


def laplace_rows(pad_ref, plane, row, lane_weights):
    at = plane + EDGE
    field = pad_ref[at, pl.ds(8 + row, SLICE), :]
    total = (3.0 * CENTRE) * field
    for index, weight in enumerate(COEFFS):
        k = index + 1
        pair = pad_ref[at + k, pl.ds(8 + row, SLICE), :] + pad_ref[at - k, pl.ds(8 + row, SLICE), :]
        pair = pair + (pad_ref[at, pl.ds(8 + row + k, SLICE), :] + pad_ref[at, pl.ds(8 + row - k, SLICE), :])
        total = total + weight * pair
        total = total + lane_weights[2 * index] * pltpu.roll(field, NZ - k, 1)
        total = total + lane_weights[2 * index + 1] * pltpu.roll(field, k, 1)
    return field, total


def make_lane_weights():
    lane = lax.broadcasted_iota(jnp.int32, (SLICE, NZ), 1)
    out = []
    for index, weight in enumerate(COEFFS):
        k = index + 1
        out.append(jnp.where(lane < NZ - k, weight, 0.0))
        out.append(jnp.where(lane >= k, weight, 0.0))
    return out


def own_kernel(forward, tick, has_extra, *refs):
    refs = list(refs)
    take = lambda n: [refs.pop(0) for _ in range(n)]
    first_ref = take(1)[0]
    if not forward or tick > 0:
        receivers_ref, lists_ref = take(2)
    if forward:
        source_ref, wavelet_ref = take(2)
    observed = take(1)[0] if (forward and tick > 0) or (not forward and tick == STEPS - 1) else None
    cur = take(3)
    old = take(3)
    model = take(3)
    if not forward:
        if tick == STEPS - 1:
            last = take(3)
        else:
            res_in = take(1)[0]
        if has_extra:
            image = take(3)
            grad_in = take(1)[0]
    next_mid, base_lo, base_hi = take(3)
    if forward:
        image_out = take(3)
        res_out = take(1)[0] if tick > 0 else None
    else:
        res_out = take(1)[0] if tick == STEPS - 1 else None
        grad_out = take(1)[0] if has_extra or tick == STEPS - 1 else None
    pad_ref = take(1)[0]

    fill_padded(pad_ref, *cur)
    weights = make_lane_weights()
    outs = (base_lo, next_mid, base_hi)
    low = 0
    for region, count in enumerate((EDGE, MID, EDGE)):

        def body(i, carry, region=region, low=low):
            for row in range(0, NY, SLICE):
                field, total = laplace_rows(pad_ref, low + i, row, weights)
                rows = pl.ds(row, SLICE)
                value = 2.0 * field - old[region][i, rows, :] + model[region][i, rows, :] * total
                outs[region][i, rows, :] = value
                if forward:
                    image_out[region][i, rows, :] = total
                elif has_extra:
                    grad_out[low + i, rows, :] = grad_in[low + i, rows, :] + field * image[region][i, rows, :]
                elif grad_out is not None:
                    grad_out[low + i, rows, :] = jnp.zeros((SLICE, NZ), jnp.float32)
            return carry

        lax.fori_loop(0, count, body, 0)
        low += count

    if forward:
        add_source(first_ref, source_ref, wavelet_ref, tick, next_mid, EDGE, MID)
        if tick > 0:
            take_residuals(first_ref, receivers_ref, lists_ref, observed, tick - 1, cur, res_out)
    else:
        if tick == STEPS - 1:
            take_residuals(first_ref, receivers_ref, lists_ref, observed, tick, last, res_out)
            res_in = res_out
        add_residuals(first_ref, receivers_ref, lists_ref, res_in, next_mid, 1, EDGE)


def edge_kernel(forward, tick, high, *refs):
    refs = list(refs)
    take = lambda n: [refs.pop(0) for _ in range(n)]
    first_ref = take(1)[0]
    if forward:
        source_ref, wavelet_ref = take(2)
    else:
        receivers_ref, lists_ref = take(2)
    halo, base, model = take(3)
    if forward:
        part = take(1)[0]
    else:
        res_ref = take(1)[0]
    take(1)
    edge = take(1)[0]
    if forward:
        image = take(1)[0]

    def body(c, carry):
        rows = pl.ds(pl.multiple_of(c * CHUNK, CHUNK), CHUNK)
        far = [halo[i, rows, :] for i in range(EDGE)]
        if not high:
            far = far[::-1]
        for j in range(EDGE):
            extra = COEFFS[3] * far[j]
            for k in range(j + 1, 4):
                extra = extra + COEFFS[k - 1] * far[EDGE + j - k]
            at = EDGE - 1 - j if high else j
            edge[at, rows, :] = base[at, rows, :] + model[at, rows, :] * extra
            if forward:
                image[at, rows, :] = part[at, rows, :] + extra
        return carry

    lax.fori_loop(0, NY // CHUNK, body, 0)
    low = ROWS - EDGE if high else 0
    if forward:
        add_source(first_ref, source_ref, wavelet_ref, tick, edge, low, EDGE)
    else:
        add_residuals(first_ref, receivers_ref, lists_ref, res_ref, edge, 2 if high else 0, low)


def swap(value, axis, pairs):
    return lax.ppermute(value, axis, pairs)


def shot_sum(grad):
    shot = lax.axis_index("shot")
    core = shot % 2
    y = (shot // 2) % 4
    other_core = [(k, k ^ 1) for k in range(16)]
    other_z = [(k, k ^ 8) for k in range(16)]

    def turn(r):
        return [(k, (k // 8) * 8 + ((k // 2 + r) % 4) * 2 + k % 2) for k in range(16)]

    keep = lax.dynamic_slice_in_dim(grad, core * 8, 8, 0)
    send = lax.dynamic_slice_in_dim(grad, (1 - core) * 8, 8, 0)
    half = keep + swap(send, "shot", other_core)
    parts = [lax.dynamic_slice_in_dim(half, ((y + r) % 4) * 2, 2, 0) for r in range(4)]
    got = [swap(parts[r], "shot", turn(r)) for r in (1, 2, 3)]
    part = parts[0] + got[0] + got[1] + got[2]
    part = part + swap(part, "shot", other_z)
    got = [part] + [swap(part, "shot", turn(r)) for r in (1, 2, 3)]
    half = jnp.zeros((8, NY, NZ), jnp.float32)
    for r in range(4):
        half = lax.dynamic_update_slice_in_dim(half, got[r], ((y - r) % 4) * 2, 0)
    other = swap(half, "shot", other_core)
    first = jnp.where(core == 0, half, other)
    second = jnp.where(core == 0, other, half)
    return jnp.concatenate([first, second])


def dom_max(value):
    value = jnp.broadcast_to(value, (8, 128))

    def along_x(r):
        return [(k, ((k // 4 + r) % 4) * 4 + k % 4) for k in range(16)]

    def along_z(r):
        return [(k, (k // 4) * 4 + (k + r) % 4) for k in range(16)]

    for turn in (along_x, along_z):
        got = [swap(value, "dom", turn(r)) for r in (1, 2, 3)]
        value = jnp.maximum(jnp.maximum(value, got[0]), jnp.maximum(got[1], got[2]))
    return value[0, 0]


def on_device(model_slab, wave_prev, wave_now, adjoint_next, adjoint_now, wavelet, source_cell, receiver_cells, observed):
    ends = [(i, i ^ 1) for i in range(16)]
    starts = [(i, i + 1 if i % 2 else i - 1) for i in range(1, 15)]
    place = lax.axis_index("dom")

    first = jnp.stack([place * (ROWS * NY * NZ), place % 2]).astype(jnp.int32)

    def cut(a):
        return call(
            cut_kernel,
            [planes(EDGE), planes(MID), planes(EDGE)],
            [],
            [SMEM, VMEM],
            [VMEM] * 3,
            1000,
            2 * ROWS * NY * NZ * 4,
            "cut",
        )(first, a)

    lists = call(
        sort_kernel,
        jax.ShapeDtypeStruct((4, REC + 128), jnp.int32),
        [],
        [SMEM, SMEM],
        SMEM,
        1000,
        4096,
        "sort_receivers",
    )(first, receiver_cells)
    observed = observed[0]
    model = cut(model_slab)
    pad = [pltpu.VMEM((ROWS + 2 * EDGE, NY + 16, NZ), jnp.float32)]
    res_shape = jax.ShapeDtypeStruct((REC, NZ), jnp.float32)
    own_cost = dict(flops=ROWS * NY * NZ * 60, nbytes=8 * ROWS * NY * NZ * 4)
    edge_cost = dict(flops=EDGE * NY * NZ * 10, nbytes=6 * EDGE * NY * NZ * 4)
    ANY = pl.BlockSpec(memory_space=pl.ANY)
    source = (first, source_cell, wavelet)
    taken = (first, receiver_cells, lists)

    def edges(forward, tick, sent, bases, parts):
        outs = [None, None]
        done = bases[0]
        for high in (True, False):
            side = 2 if high else 0
            smem = source if forward else taken
            outs[high] = call(
                functools.partial(edge_kernel, forward, tick, high),
                [planes(EDGE)] * (2 if forward else 1),
                [],
                [SMEM] * 3 + [VMEM] * 4 + [ANY],
                [VMEM] * (2 if forward else 1),
                name="edge_high" if high else "edge_low",
                **edge_cost,
            )(*smem, sent[high], bases[high], model[side], parts[high], done)
            done = outs[high][0]
        return outs

    def halos(cur, tick):
        low = swap(cur[0], "dom", starts)
        high = swap(cur[2], "dom", ends)
        return low, high

    old, cur = cut(wave_prev[0]), cut(wave_now[0])
    images, residuals = [], []
    for tick in range(STEPS):
        sent = halos(cur, tick)
        extra = (observed,) if tick > 0 else ()
        smem = ((first, receiver_cells, lists) if tick > 0 else (first,)) + (source_cell, wavelet) + extra
        outs = [planes(MID), planes(EDGE), planes(EDGE), planes(EDGE), planes(MID), planes(EDGE)]
        outs += [res_shape] if tick > 0 else []
        result = call(
            functools.partial(own_kernel, True, tick, False),
            outs,
            pad,
            [SMEM] * len(smem) + [VMEM] * 9,
            [VMEM] * len(outs),
            name="own_forward",
            **own_cost,
        )(*smem, *cur, *old, *model)
        mid, base_lo, base_hi, part_lo, image_mid, part_hi = result[:6]
        if tick > 0:
            residuals.append(result[6])
        (low, image_lo), (high, image_hi) = edges(True, tick, sent, (base_lo, base_hi), (part_lo, part_hi))
        images.append((image_lo, image_mid, image_hi))
        old, cur = cur, (low, mid, high)
    last = cur
    old, cur = cut(adjoint_next[0]), cut(adjoint_now[0])
    grad = None
    for tick in reversed(range(STEPS)):
        sent = halos(cur, tick)
        top = tick == STEPS - 1
        extra = (observed,) if top else ()
        fields = last if top else (residuals[tick], *images[tick + 1], grad)
        outs = [planes(MID), planes(EDGE), planes(EDGE)]
        outs += [res_shape] if top else []
        outs += [planes(ROWS)]
        result = call(
            functools.partial(own_kernel, False, tick, not top),
            outs,
            pad,
            [SMEM] * (3 + len(extra)) + [VMEM] * (9 + len(fields)),
            [VMEM] * len(outs),
            name="own_adjoint",
            **own_cost,
        )(*taken, *extra, *cur, *old, *model, *fields)
        mid, base_lo, base_hi = result[:3]
        if top:
            residuals.append(result[3])
        grad = result[-1]
        (low,), (high,) = edges(False, tick, sent, (base_lo, base_hi), (residuals[tick],) * 2)
        old, cur = cur, (low, mid, high)
    grad = call(
        join_kernel,
        planes(ROWS),
        [],
        [SMEM] + [VMEM] * 7,
        VMEM,
        2 * ROWS * NY * NZ,
        4 * ROWS * NY * NZ * 4,
        "join",
    )(first, grad, *cur, *images[0])
    total = shot_sum(grad)
    peak = dom_max(jnp.max(jnp.abs(total)))
    direction = total / (peak + EPSILON)
    new_model = model_slab * (1.0 - STEP_FRACTION * direction)
    return direction, new_model


def solution(mesh):
    placed = (
        P("dom", None, None),
        P("shot", "dom", None, None),
        P("shot", "dom", None, None),
        P("shot", "dom", None, None),
        P("shot", "dom", None, None),
        P("shot", None),
        P("shot"),
        P("shot", None),
        P("shot", None, None),
    )
    return jax.shard_map(
        on_device,
        mesh=mesh,
        in_specs=placed,
        out_specs=(P("dom", None, None), P("dom", None, None)),
        check_vma=False,
    )
```

```python
import functools
import jax
import jax.numpy as jnp
from jax import lax
from jax.experimental import pallas as pl
from jax.experimental.pallas import tpu as pltpu
from jax.sharding import PartitionSpec as P

STEPS = 8
COEFFS = (8.0 / 5.0, -1.0 / 5.0, 8.0 / 315.0, -1.0 / 560.0)
CENTRE = -205.0 / 72.0
STEP_FRACTION = 0.1
EPSILON = 1e-06
ROWS = 16
NY = 128
NZ = 128
REC = 256
EDGE = 4
MID = ROWS - 2 * EDGE
CHUNK = 32
SLICE = 8
EARLY = (4, 6)
VMEM = pl.BlockSpec(memory_space=pltpu.VMEM)
SMEM = pl.BlockSpec(memory_space=pltpu.SMEM)
LIMIT = 12 * 1024 * 1024


def planes(count):
    return jax.ShapeDtypeStruct((count, NY, NZ), jnp.float32)


def call(kernel, outs, scratch, specs, out_specs, flops, nbytes, name, aliases={}):
    return pl.pallas_call(
        kernel,
        out_shape=outs,
        in_specs=specs,
        out_specs=out_specs,
        scratch_shapes=scratch,
        input_output_aliases=aliases,
        compiler_params=pltpu.CompilerParams(vmem_limit_bytes=LIMIT),
        cost_estimate=pl.CostEstimate(flops=flops, transcendentals=0, bytes_accessed=nbytes),
        name=name,
    )


def sort_receivers(first, receivers):
    plane = where_of(receivers, first)[0]
    bounds = jnp.array([0, EDGE, ROWS - EDGE, ROWS], jnp.int32)
    inside = (plane[None] >= bounds[:3, None]) & (plane[None] < bounds[1:, None])
    order = jnp.arange(REC, dtype=jnp.int32)
    ahead = inside[:, :, None] & (order[:, None] < order[None])[None]
    rank = jnp.sum(ahead.astype(jnp.int32), 1)
    hit = inside[:, :, None] & (rank[:, :, None] == order[None, None])
    lists = jnp.sum(jnp.where(hit, order[None, :, None], 0), 1)
    counts = jnp.sum(inside.astype(jnp.int32), 1)
    return jnp.concatenate([lists, jnp.broadcast_to(counts[:, None], (3, 128))], 1)


def where_of(cell, first_ref):
    local = cell - first_ref[0]
    plane = local >> 14
    plane = jnp.where(first_ref[1] == 1, ROWS - 1 - plane, plane)
    return plane, (local >> 7) & 127, local & 127


def cut_kernel(first_ref, whole_ref, low_ref, mid_ref, high_ref):
    start = 0
    for ref, count in ((low_ref, EDGE), (mid_ref, MID), (high_ref, EDGE)):

        def body(i, carry, ref=ref, start=start):
            plane = jnp.where(first_ref[1] == 1, ROWS - 1 - start - i, start + i)
            ref[i] = whole_ref[plane]
            return carry

        lax.fori_loop(0, count, body, 0)
        start += count


def join_kernel(first_ref, grad_ref, a_low, a_mid, a_high, b_low, b_mid, b_high, out_ref):
    start = 0
    for a, b, count in ((a_low, b_low, EDGE), (a_mid, b_mid, MID), (a_high, b_high, EDGE)):

        def body(i, carry, a=a, b=b, start=start):
            plane = jnp.where(first_ref[1] == 1, ROWS - 1 - start - i, start + i)
            out_ref[plane] = grad_ref[start + i] + a[i] * b[i]
            return carry

        lax.fori_loop(0, count, body, 0)
        start += count


def largest_kernel(core_ref, half_ref, other_ref, total_ref, out_ref):
    def body(i, best):
        for ref, half in ((half_ref, core_ref[0]), (other_ref, 1 - core_ref[0])):
            for row in range(0, NY, 8):
                rows = pl.ds(row, 8)
                value = ref[i, rows, :]
                total_ref[half * 8 + i, rows, :] = value
                best = jnp.maximum(best, jnp.abs(value))
        return best

    out_ref[...] = lax.fori_loop(0, 8, body, jnp.zeros((8, NZ), jnp.float32))


def final_kernel(largest_ref, total_ref, model_ref, direction_ref, new_ref):
    bottom = jnp.max(largest_ref[...]) + EPSILON
    direction = total_ref[...] / bottom
    direction_ref[...] = direction
    new_ref[...] = model_ref[...] * (1.0 - STEP_FRACTION * direction)


def lanes_row():
    return lax.broadcasted_iota(jnp.int32, (1, NZ), 1)


def add_source(first_ref, source_ref, wavelet_ref, tick, ref, low, count):
    plane, row, lane = where_of(source_ref[0], first_ref)
    plane = plane - low

    @pl.when((plane >= 0) & (plane < count))
    def _():
        extra = jnp.where(lanes_row() == lane, wavelet_ref[0, tick], 0.0)
        spot = ref[plane, pl.ds(row, 1), :]
        ref[plane, pl.ds(row, 1), :] = spot + extra


def add_residuals(first_ref, receivers_ref, lists_ref, res_ref, ref, region, low):
    def body(i, carry):
        j = lists_ref[region, i]
        plane, row, lane = where_of(receivers_ref[0, j], first_ref)
        spot = ref[plane - low, pl.ds(row, 1), :]
        ref[plane - low, pl.ds(row, 1), :] = spot + res_ref[pl.ds(j, 1), :]
        return carry

    lax.fori_loop(0, lists_ref[region, REC], body, 0)


def take_residuals(first_ref, receivers_ref, lists_ref, observed_ref, tick, refs, res_ref):
    lows = (0, EDGE, ROWS - EDGE)
    for region in range(3):
        ref, low = refs[region], lows[region]

        def body(i, carry):
            j = lists_ref[region, i]
            plane, row, lane = where_of(receivers_ref[0, j], first_ref)
            spot = ref[plane - low, pl.ds(row, 1), :]
            value = spot - observed_ref[tick, j]
            res_ref[pl.ds(j, 1), :] = jnp.where(lanes_row() == lane, value, 0.0)
            return carry

        lax.fori_loop(0, lists_ref[region, REC], body, 0)


def fill_padded(pad_ref, lo_ref, mid_ref, hi_ref):
    zeros = jnp.zeros((8, NZ), jnp.float32)
    for i in range(EDGE):
        pad_ref[i] = jnp.zeros((NY + 16, NZ), jnp.float32)
        pad_ref[ROWS + EDGE + i] = jnp.zeros((NY + 16, NZ), jnp.float32)
    start = EDGE
    for ref, count in ((lo_ref, EDGE), (mid_ref, MID), (hi_ref, EDGE)):

        def body(i, carry, ref=ref, start=start):
            pad_ref[start + i, pl.ds(0, 8), :] = zeros
            pad_ref[start + i, pl.ds(NY + 8, 8), :] = zeros
            pad_ref[start + i, pl.ds(8, NY), :] = ref[i]
            return carry

        lax.fori_loop(0, count, body, 0)
        start += count


def laplace_rows(pad_ref, plane, row, lane_weights):
    at = plane + EDGE
    field = pad_ref[at, pl.ds(8 + row, SLICE), :]
    total = (3.0 * CENTRE) * field
    for index, weight in enumerate(COEFFS):
        k = index + 1
        pair = pad_ref[at + k, pl.ds(8 + row, SLICE), :] + pad_ref[at - k, pl.ds(8 + row, SLICE), :]
        pair = pair + (pad_ref[at, pl.ds(8 + row + k, SLICE), :] + pad_ref[at, pl.ds(8 + row - k, SLICE), :])
        total = total + weight * pair
        total = total + lane_weights[2 * index] * pltpu.roll(field, NZ - k, 1)
        total = total + lane_weights[2 * index + 1] * pltpu.roll(field, k, 1)
    return field, total


def make_lane_weights():
    lane = lax.broadcasted_iota(jnp.int32, (SLICE, NZ), 1)
    out = []
    for index, weight in enumerate(COEFFS):
        k = index + 1
        out.append(jnp.where(lane < NZ - k, weight, 0.0))
        out.append(jnp.where(lane >= k, weight, 0.0))
    return out


def own_kernel(forward, tick, has_extra, *refs):
    refs = list(refs)
    take = lambda n: [refs.pop(0) for _ in range(n)]
    first_ref = take(1)[0]
    if not forward or tick > 0:
        receivers_ref, lists_ref = take(2)
    if forward:
        source_ref, wavelet_ref = take(2)
    observed = take(1)[0] if (forward and tick > 0) or (not forward and tick == STEPS - 1) else None
    cur = take(3)
    old = take(3)
    model = take(3)
    if forward and tick in EARLY:
        take(1)
    if not forward:
        if tick == STEPS - 1:
            last = take(3)
        else:
            res_in = take(1)[0]
        if has_extra:
            image = take(3)
            grad_in = take(1)[0]
    next_mid, base_lo, base_hi = take(3)
    if forward:
        image_out = take(3)
        res_out = take(1)[0] if tick > 0 else None
    else:
        res_out = take(1)[0] if tick == STEPS - 1 else None
        grad_out = take(1)[0] if has_extra or tick == STEPS - 1 else None
    pad_ref = take(1)[0]

    fill_padded(pad_ref, *cur)
    weights = make_lane_weights()
    outs = (base_lo, next_mid, base_hi)
    low = 0
    for region, count in enumerate((EDGE, MID, EDGE)):

        def body(i, carry, region=region, low=low):
            for row in range(0, NY, SLICE):
                field, total = laplace_rows(pad_ref, low + i, row, weights)
                rows = pl.ds(row, SLICE)
                value = 2.0 * field - old[region][i, rows, :] + model[region][i, rows, :] * total
                outs[region][i, rows, :] = value
                if forward:
                    image_out[region][i, rows, :] = total
                elif has_extra:
                    grad_out[low + i, rows, :] = grad_in[low + i, rows, :] + field * image[region][i, rows, :]
                elif grad_out is not None:
                    grad_out[low + i, rows, :] = jnp.zeros((SLICE, NZ), jnp.float32)
            return carry

        lax.fori_loop(0, count, body, 0)
        low += count

    if forward:
        add_source(first_ref, source_ref, wavelet_ref, tick, next_mid, EDGE, MID)
        if tick > 0:
            take_residuals(first_ref, receivers_ref, lists_ref, observed, tick - 1, cur, res_out)
    else:
        if tick == STEPS - 1:
            take_residuals(first_ref, receivers_ref, lists_ref, observed, tick, last, res_out)
            res_in = res_out
        add_residuals(first_ref, receivers_ref, lists_ref, res_in, next_mid, 1, EDGE)


def edge_kernel(forward, tick, high, *refs):
    refs = list(refs)
    take = lambda n: [refs.pop(0) for _ in range(n)]
    first_ref = take(1)[0]
    if forward:
        source_ref, wavelet_ref = take(2)
    else:
        receivers_ref, lists_ref = take(2)
    halo, base, model = take(3)
    if forward:
        part = take(1)[0]
    else:
        res_ref = take(1)[0]
    take(1)
    edge = take(1)[0]
    if forward:
        image = take(1)[0]

    def body(c, carry):
        rows = pl.ds(pl.multiple_of(c * CHUNK, CHUNK), CHUNK)
        far = [halo[i, rows, :] for i in range(EDGE)]
        if not high:
            far = far[::-1]
        for j in range(EDGE):
            extra = COEFFS[3] * far[j]
            for k in range(j + 1, 4):
                extra = extra + COEFFS[k - 1] * far[EDGE + j - k]
            at = EDGE - 1 - j if high else j
            edge[at, rows, :] = base[at, rows, :] + model[at, rows, :] * extra
            if forward:
                image[at, rows, :] = part[at, rows, :] + extra
        return carry

    lax.fori_loop(0, NY // CHUNK, body, 0)
    low = ROWS - EDGE if high else 0
    if forward:
        add_source(first_ref, source_ref, wavelet_ref, tick, edge, low, EDGE)
    else:
        add_residuals(first_ref, receivers_ref, lists_ref, res_ref, edge, 2 if high else 0, low)


def swap(value, axis, pairs):
    return lax.ppermute(value, axis, pairs)


def shot_sum(grad):
    shot = lax.axis_index("shot")
    core = shot % 2
    y = (shot // 2) % 4
    other_core = [(k, k ^ 1) for k in range(16)]
    other_z = [(k, k ^ 8) for k in range(16)]

    def turn(r):
        return [(k, (k // 8) * 8 + ((k // 2 + r) % 4) * 2 + k % 2) for k in range(16)]

    keep = lax.dynamic_slice_in_dim(grad, core * 8, 8, 0)
    send = lax.dynamic_slice_in_dim(grad, (1 - core) * 8, 8, 0)
    half = keep + swap(send, "shot", other_core)
    parts = [lax.dynamic_slice_in_dim(half, ((y + r) % 4) * 2, 2, 0) for r in range(4)]
    got = [swap(parts[r], "shot", turn(r)) for r in (1, 2, 3)]
    part = parts[0] + got[0] + got[1] + got[2]
    part = part + swap(part, "shot", other_z)
    got = [part] + [swap(part, "shot", turn(r)) for r in (1, 2, 3)]
    half = jnp.zeros((8, NY, NZ), jnp.float32)
    for r in range(4):
        half = lax.dynamic_update_slice_in_dim(half, got[r], ((y - r) % 4) * 2, 0)
    other = swap(half, "shot", other_core)
    return call(
        largest_kernel,
        [planes(ROWS), jax.ShapeDtypeStruct((8, NZ), jnp.float32)],
        [],
        [SMEM, VMEM, VMEM],
        [VMEM] * 2,
        2 * ROWS * NY * NZ,
        2 * ROWS * NY * NZ * 4,
        "largest",
    )(core.astype(jnp.int32).reshape(1), half, other)


def dom_max(value):
    def along_x(r):
        return [(k, ((k // 4 + r) % 4) * 4 + k % 4) for k in range(16)]

    def along_z(r):
        return [(k, (k // 4) * 4 + (k + r) % 4) for k in range(16)]

    for turn in (along_x, along_z):
        got = [swap(value, "dom", turn(r)) for r in (1, 2, 3)]
        value = jnp.maximum(jnp.maximum(value, got[0]), jnp.maximum(got[1], got[2]))
    return value


def on_device(model_slab, wave_prev, wave_now, adjoint_next, adjoint_now, wavelet, source_cell, receiver_cells, observed):
    ends = [(i, i ^ 1) for i in range(16)]
    starts = [(i, i + 1 if i % 2 else i - 1) for i in range(1, 15)]
    place = lax.axis_index("dom")

    first = jnp.stack([place * (ROWS * NY * NZ), place % 2]).astype(jnp.int32)

    def cut(a):
        return call(
            cut_kernel,
            [planes(EDGE), planes(MID), planes(EDGE)],
            [],
            [SMEM, VMEM],
            [VMEM] * 3,
            1000,
            2 * ROWS * NY * NZ * 4,
            "cut",
        )(first, a)

    lists = sort_receivers(first, receiver_cells[0])
    observed = observed[0]
    model = cut(model_slab)
    pad = [pltpu.VMEM((ROWS + 2 * EDGE, NY + 16, NZ), jnp.float32)]
    res_shape = jax.ShapeDtypeStruct((REC, NZ), jnp.float32)
    own_cost = dict(flops=ROWS * NY * NZ * 60, nbytes=8 * ROWS * NY * NZ * 4)
    edge_cost = dict(flops=EDGE * NY * NZ * 10, nbytes=6 * EDGE * NY * NZ * 4)
    ANY = pl.BlockSpec(memory_space=pl.ANY)
    source = (first, source_cell, wavelet)
    taken = (first, receiver_cells, lists)

    def edges(forward, tick, sent, bases, parts):
        outs = [None, None]
        done = bases[0]
        for high in (True, False):
            side = 2 if high else 0
            smem = source if forward else taken
            outs[high] = call(
                functools.partial(edge_kernel, forward, tick, high),
                [planes(EDGE)] * (2 if forward else 1),
                [],
                [SMEM] * 3 + [VMEM] * 4 + [ANY],
                [VMEM] * (2 if forward else 1),
                name="edge_high" if high else "edge_low",
                **edge_cost,
            )(*smem, sent[high], bases[high], model[side], parts[high], done)
            done = outs[high][0]
        return outs

    def halos(cur, tick):
        low = swap(cur[0], "dom", starts)
        high = swap(cur[2], "dom", ends)
        return low, high

    old, cur = cut(wave_prev[0]), cut(wave_now[0])
    adjoint_old, adjoint_cur = cut(adjoint_next[0]), cut(adjoint_now[0])
    adjoint_sent = [None, None]
    images, residuals = [], []
    for tick in range(STEPS):
        sent = halos(cur, tick)
        extra = (observed,) if tick > 0 else ()
        smem = ((first, receiver_cells, lists) if tick > 0 else (first,)) + (source_cell, wavelet) + extra
        outs = [planes(MID), planes(EDGE), planes(EDGE), planes(EDGE), planes(MID), planes(EDGE)]
        outs += [res_shape] if tick > 0 else []
        result = call(
            functools.partial(own_kernel, True, tick, False),
            outs,
            pad,
            [SMEM] * len(smem) + [VMEM] * 9 + [ANY] * (tick in EARLY),
            [VMEM] * len(outs),
            name="own_forward",
            **own_cost,
        )(*smem, *cur, *old, *model, *([adjoint_sent[EARLY.index(tick)]] if tick in EARLY else []))
        mid, base_lo, base_hi, part_lo, image_mid, part_hi = result[:6]
        if tick + 1 in EARLY:
            side = EARLY.index(tick + 1)
            edge, mid = lax.optimization_barrier((adjoint_cur[2 * side], mid))
            adjoint_sent[side] = swap(edge, "dom", (starts, ends)[side])
        if tick > 0:
            residuals.append(result[6])
        (low, image_lo), (high, image_hi) = edges(True, tick, sent, (base_lo, base_hi), (part_lo, part_hi))
        images.append((image_lo, image_mid, image_hi))
        old, cur = cur, (low, mid, high)
    last = cur
    old, cur = adjoint_old, adjoint_cur
    grad = None
    for tick in reversed(range(STEPS)):
        top = tick == STEPS - 1
        sent = adjoint_sent if top else halos(cur, tick)
        extra = (observed,) if top else ()
        fields = last if top else (residuals[tick], *images[tick + 1], grad)
        outs = [planes(MID), planes(EDGE), planes(EDGE)]
        outs += [res_shape] if top else []
        outs += [planes(ROWS)]
        result = call(
            functools.partial(own_kernel, False, tick, not top),
            outs,
            pad,
            [SMEM] * (3 + len(extra)) + [VMEM] * (9 + len(fields)),
            [VMEM] * len(outs),
            name="own_adjoint",
            **own_cost,
        )(*taken, *extra, *cur, *old, *model, *fields)
        mid, base_lo, base_hi = result[:3]
        if top:
            residuals.append(result[3])
        grad = result[-1]
        (low,), (high,) = edges(False, tick, sent, (base_lo, base_hi), (residuals[tick],) * 2)
        old, cur = cur, (low, mid, high)
    grad = call(
        join_kernel,
        planes(ROWS),
        [],
        [SMEM] + [VMEM] * 7,
        VMEM,
        2 * ROWS * NY * NZ,
        4 * ROWS * NY * NZ * 4,
        "join",
    )(first, grad, *cur, *images[0])
    total, largest = shot_sum(grad)
    block = pl.BlockSpec((EDGE, NY, NZ), lambda i: (i, 0, 0))
    return pl.pallas_call(
        final_kernel,
        grid=(ROWS // EDGE,),
        out_shape=[planes(ROWS)] * 2,
        in_specs=[pl.BlockSpec((8, NZ), lambda i: (0, 0)), block, block],
        out_specs=[block, block],
        compiler_params=pltpu.CompilerParams(vmem_limit_bytes=LIMIT),
        name="final",
    )(dom_max(largest), total, model_slab)


def solution(mesh):
    placed = (
        P("dom", None, None),
        P("shot", "dom", None, None),
        P("shot", "dom", None, None),
        P("shot", "dom", None, None),
        P("shot", "dom", None, None),
        P("shot", None),
        P("shot"),
        P("shot", None),
        P("shot", None, None),
    )
    return jax.shard_map(
        on_device,
        mesh=mesh,
        in_specs=placed,
        out_specs=(P("dom", None, None), P("dom", None, None)),
        check_vma=False,
    )
```

```python
import functools
import jax
import jax.numpy as jnp
from jax import lax
from jax.experimental import pallas as pl
from jax.experimental.pallas import tpu as pltpu
from jax.sharding import PartitionSpec as P

STEPS = 8
COEFFS = (8.0 / 5.0, -1.0 / 5.0, 8.0 / 315.0, -1.0 / 560.0)
CENTRE = -205.0 / 72.0
STEP_FRACTION = 0.1
EPSILON = 1e-06
ROWS = 16
NY = 128
NZ = 128
REC = 256
EDGE = 4
MID = ROWS - 2 * EDGE
CHUNK = 32
SLICE = 8
VMEM = pl.BlockSpec(memory_space=pltpu.VMEM)
SMEM = pl.BlockSpec(memory_space=pltpu.SMEM)
LIMIT = 12 * 1024 * 1024


def planes(count):
    return jax.ShapeDtypeStruct((count, NY, NZ), jnp.float32)


def call(kernel, outs, scratch, specs, out_specs, flops, nbytes, name, aliases={}):
    return pl.pallas_call(
        kernel,
        out_shape=outs,
        in_specs=specs,
        out_specs=out_specs,
        scratch_shapes=scratch,
        input_output_aliases=aliases,
        compiler_params=pltpu.CompilerParams(vmem_limit_bytes=LIMIT),
        cost_estimate=pl.CostEstimate(flops=flops, transcendentals=0, bytes_accessed=nbytes),
        name=name,
    )


def sort_kernel(first_ref, receivers_ref, lists_ref):
    def body(j, counts):
        plane = where_of(receivers_ref[0, j], first_ref)[0]
        inside = (plane >= 0) & (plane < ROWS)
        low = inside & (plane < EDGE)
        high = inside & (plane >= ROWS - EDGE)
        mid = inside & (plane >= EDGE) & (plane < ROWS - EDGE)
        lists_ref[jnp.where(low, 0, 3), counts[0]] = j
        lists_ref[jnp.where(mid, 1, 3), counts[1]] = j
        lists_ref[jnp.where(high, 2, 3), counts[2]] = j
        return tuple(c + x.astype(jnp.int32) for c, x in zip(counts, (low, mid, high)))

    zero = jnp.int32(0)
    counts = lax.fori_loop(0, REC, body, (zero, zero, zero), unroll=4)
    for region in range(3):
        lists_ref[region, REC] = counts[region]


def where_of(cell, first_ref):
    local = cell - first_ref[0]
    plane = local >> 14
    plane = jnp.where(first_ref[1] == 1, ROWS - 1 - plane, plane)
    return plane, (local >> 7) & 127, local & 127


def cut_kernel(first_ref, whole_ref, low_ref, mid_ref, high_ref):
    start = 0
    for ref, count in ((low_ref, EDGE), (mid_ref, MID), (high_ref, EDGE)):

        def body(i, carry, ref=ref, start=start):
            plane = jnp.where(first_ref[1] == 1, ROWS - 1 - start - i, start + i)
            ref[i] = whole_ref[plane]
            return carry

        lax.fori_loop(0, count, body, 0)
        start += count


def join_kernel(first_ref, grad_ref, a_low, a_mid, a_high, b_low, b_mid, b_high, out_ref):
    start = 0
    for a, b, count in ((a_low, b_low, EDGE), (a_mid, b_mid, MID), (a_high, b_high, EDGE)):

        def body(i, carry, a=a, b=b, start=start):
            plane = jnp.where(first_ref[1] == 1, ROWS - 1 - start - i, start + i)
            out_ref[plane] = grad_ref[start + i] + a[i] * b[i]
            return carry

        lax.fori_loop(0, count, body, 0)
        start += count


def lanes_row():
    return lax.broadcasted_iota(jnp.int32, (1, NZ), 1)


def add_source(first_ref, source_ref, wavelet_ref, tick, ref, low, count):
    plane, row, lane = where_of(source_ref[0], first_ref)
    plane = plane - low

    @pl.when((plane >= 0) & (plane < count))
    def _():
        extra = jnp.where(lanes_row() == lane, wavelet_ref[0, tick], 0.0)
        spot = ref[plane, pl.ds(row, 1), :]
        ref[plane, pl.ds(row, 1), :] = spot + extra


def add_residuals(first_ref, receivers_ref, lists_ref, res_ref, ref, region, low):
    def body(i, carry):
        j = lists_ref[region, i]
        plane, row, lane = where_of(receivers_ref[0, j], first_ref)
        spot = ref[plane - low, pl.ds(row, 1), :]
        ref[plane - low, pl.ds(row, 1), :] = spot + res_ref[pl.ds(j, 1), :]
        return carry

    lax.fori_loop(0, lists_ref[region, REC], body, 0)


def take_residuals(first_ref, receivers_ref, lists_ref, observed_ref, tick, refs, res_ref):
    lows = (0, EDGE, ROWS - EDGE)
    for region in range(3):
        ref, low = refs[region], lows[region]

        def body(i, carry):
            j = lists_ref[region, i]
            plane, row, lane = where_of(receivers_ref[0, j], first_ref)
            spot = ref[plane - low, pl.ds(row, 1), :]
            value = spot - observed_ref[tick, j]
            res_ref[pl.ds(j, 1), :] = jnp.where(lanes_row() == lane, value, 0.0)
            return carry

        lax.fori_loop(0, lists_ref[region, REC], body, 0)


def fill_padded(pad_ref, lo_ref, mid_ref, hi_ref):
    zeros = jnp.zeros((8, NZ), jnp.float32)
    for i in range(EDGE):
        pad_ref[i] = jnp.zeros((NY + 16, NZ), jnp.float32)
        pad_ref[ROWS + EDGE + i] = jnp.zeros((NY + 16, NZ), jnp.float32)
    start = EDGE
    for ref, count in ((lo_ref, EDGE), (mid_ref, MID), (hi_ref, EDGE)):

        def body(i, carry, ref=ref, start=start):
            pad_ref[start + i, pl.ds(0, 8), :] = zeros
            pad_ref[start + i, pl.ds(NY + 8, 8), :] = zeros
            pad_ref[start + i, pl.ds(8, NY), :] = ref[i]
            return carry

        lax.fori_loop(0, count, body, 0)
        start += count


def lane_matrix():
    away = jnp.abs(lax.broadcasted_iota(jnp.int32, (NZ, NZ), 0) - lax.broadcasted_iota(jnp.int32, (NZ, NZ), 1))
    out = jnp.zeros((NZ, NZ), jnp.float32)
    for k, weight in enumerate((8064.0, -1008.0, 128.0, -9.0)):
        out = jnp.where(away == k + 1, weight, out)
    return out.astype(jnp.bfloat16)


def lane_terms(plane, matrix):
    total = None
    for piece in range(3):
        part = plane.astype(jnp.bfloat16)
        plane = plane - part.astype(jnp.float32)
        term = jnp.dot(part, matrix, preferred_element_type=jnp.float32)
        total = term if total is None else total + term
    return total * (1.0 / 5040.0)


def laplace_rows(pad_ref, plane, row, along):
    at = plane + EDGE
    field = pad_ref[at, pl.ds(8 + row, SLICE), :]
    total = (3.0 * CENTRE) * field + along[row : row + SLICE]
    for index, weight in enumerate(COEFFS):
        k = index + 1
        pair = pad_ref[at + k, pl.ds(8 + row, SLICE), :] + pad_ref[at - k, pl.ds(8 + row, SLICE), :]
        pair = pair + (pad_ref[at, pl.ds(8 + row + k, SLICE), :] + pad_ref[at, pl.ds(8 + row - k, SLICE), :])
        total = total + weight * pair
    return field, total


def own_kernel(forward, tick, has_extra, *refs):
    refs = list(refs)
    take = lambda n: [refs.pop(0) for _ in range(n)]
    first_ref = take(1)[0]
    if not forward or tick > 0:
        receivers_ref, lists_ref = take(2)
    if forward:
        source_ref, wavelet_ref = take(2)
    observed = take(1)[0] if (forward and tick > 0) or (not forward and tick == STEPS - 1) else None
    cur = take(3)
    old = take(3)
    model = take(3)
    if not forward:
        if tick == STEPS - 1:
            last = take(3)
        else:
            res_in = take(1)[0]
        if has_extra:
            image = take(3)
            grad_in = take(1)[0]
    next_mid, base_lo, base_hi = take(3)
    if forward:
        image_out = take(3)
        res_out = take(1)[0] if tick > 0 else None
    else:
        res_out = take(1)[0] if tick == STEPS - 1 else None
        grad_out = take(1)[0] if has_extra or tick == STEPS - 1 else None
    pad_ref = take(1)[0]

    fill_padded(pad_ref, *cur)
    matrix = lane_matrix()
    outs = (base_lo, next_mid, base_hi)
    low = 0
    for region, count in enumerate((EDGE, MID, EDGE)):

        def body(i, carry, region=region, low=low):
            along = lane_terms(cur[region][i], matrix)
            for row in range(0, NY, SLICE):
                field, total = laplace_rows(pad_ref, low + i, row, along)
                rows = pl.ds(row, SLICE)
                value = 2.0 * field - old[region][i, rows, :] + model[region][i, rows, :] * total
                outs[region][i, rows, :] = value
                if forward:
                    image_out[region][i, rows, :] = total
                elif has_extra:
                    grad_out[low + i, rows, :] = grad_in[low + i, rows, :] + field * image[region][i, rows, :]
                elif grad_out is not None:
                    grad_out[low + i, rows, :] = jnp.zeros((SLICE, NZ), jnp.float32)
            return carry

        lax.fori_loop(0, count, body, 0)
        low += count

    if forward:
        add_source(first_ref, source_ref, wavelet_ref, tick, next_mid, EDGE, MID)
        if tick > 0:
            take_residuals(first_ref, receivers_ref, lists_ref, observed, tick - 1, cur, res_out)
    else:
        if tick == STEPS - 1:
            take_residuals(first_ref, receivers_ref, lists_ref, observed, tick, last, res_out)
            res_in = res_out
        add_residuals(first_ref, receivers_ref, lists_ref, res_in, next_mid, 1, EDGE)


def edge_kernel(forward, tick, high, *refs):
    refs = list(refs)
    take = lambda n: [refs.pop(0) for _ in range(n)]
    first_ref = take(1)[0]
    if forward:
        source_ref, wavelet_ref = take(2)
    else:
        receivers_ref, lists_ref = take(2)
    halo, base, model = take(3)
    if forward:
        part = take(1)[0]
    else:
        res_ref = take(1)[0]
    take(1)
    edge = take(1)[0]
    if forward:
        image = take(1)[0]

    def body(c, carry):
        rows = pl.ds(pl.multiple_of(c * CHUNK, CHUNK), CHUNK)
        far = [halo[i, rows, :] for i in range(EDGE)]
        if not high:
            far = far[::-1]
        for j in range(EDGE):
            extra = COEFFS[3] * far[j]
            for k in range(j + 1, 4):
                extra = extra + COEFFS[k - 1] * far[EDGE + j - k]
            at = EDGE - 1 - j if high else j
            edge[at, rows, :] = base[at, rows, :] + model[at, rows, :] * extra
            if forward:
                image[at, rows, :] = part[at, rows, :] + extra
        return carry

    lax.fori_loop(0, NY // CHUNK, body, 0)
    low = ROWS - EDGE if high else 0
    if forward:
        add_source(first_ref, source_ref, wavelet_ref, tick, edge, low, EDGE)
    else:
        add_residuals(first_ref, receivers_ref, lists_ref, res_ref, edge, 2 if high else 0, low)


def swap(value, axis, pairs):
    return lax.ppermute(value, axis, pairs)


def shot_sum(grad):
    shot = lax.axis_index("shot")
    core = shot % 2
    y = (shot // 2) % 4
    other_core = [(k, k ^ 1) for k in range(16)]
    other_z = [(k, k ^ 8) for k in range(16)]

    def turn(r):
        return [(k, (k // 8) * 8 + ((k // 2 + r) % 4) * 2 + k % 2) for k in range(16)]

    keep = lax.dynamic_slice_in_dim(grad, core * 8, 8, 0)
    send = lax.dynamic_slice_in_dim(grad, (1 - core) * 8, 8, 0)
    half = keep + swap(send, "shot", other_core)
    parts = [lax.dynamic_slice_in_dim(half, ((y + r) % 4) * 2, 2, 0) for r in range(4)]
    got = [swap(parts[r], "shot", turn(r)) for r in (1, 2, 3)]
    part = parts[0] + got[0] + got[1] + got[2]
    part = part + swap(part, "shot", other_z)
    got = [part] + [swap(part, "shot", turn(r)) for r in (1, 2, 3)]
    half = jnp.zeros((8, NY, NZ), jnp.float32)
    for r in range(4):
        half = lax.dynamic_update_slice_in_dim(half, got[r], ((y - r) % 4) * 2, 0)
    other = swap(half, "shot", other_core)
    first = jnp.where(core == 0, half, other)
    second = jnp.where(core == 0, other, half)
    return jnp.concatenate([first, second])


def dom_max(value):
    value = jnp.broadcast_to(value, (8, 128))

    def along_x(r):
        return [(k, ((k // 4 + r) % 4) * 4 + k % 4) for k in range(16)]

    def along_z(r):
        return [(k, (k // 4) * 4 + (k + r) % 4) for k in range(16)]

    for turn in (along_x, along_z):
        got = [swap(value, "dom", turn(r)) for r in (1, 2, 3)]
        value = jnp.maximum(jnp.maximum(value, got[0]), jnp.maximum(got[1], got[2]))
    return value[0, 0]


def on_device(model_slab, wave_prev, wave_now, adjoint_next, adjoint_now, wavelet, source_cell, receiver_cells, observed):
    ends = [(i, i ^ 1) for i in range(16)]
    starts = [(i, i + 1 if i % 2 else i - 1) for i in range(1, 15)]
    place = lax.axis_index("dom")

    first = jnp.stack([place * (ROWS * NY * NZ), place % 2]).astype(jnp.int32)

    def cut(a):
        return call(
            cut_kernel,
            [planes(EDGE), planes(MID), planes(EDGE)],
            [],
            [SMEM, VMEM],
            [VMEM] * 3,
            1000,
            2 * ROWS * NY * NZ * 4,
            "cut",
        )(first, a)

    lists = call(
        sort_kernel,
        jax.ShapeDtypeStruct((4, REC + 128), jnp.int32),
        [],
        [SMEM, SMEM],
        SMEM,
        1000,
        4096,
        "sort_receivers",
    )(first, receiver_cells)
    observed = observed[0]
    model = cut(model_slab)
    pad = [pltpu.VMEM((ROWS + 2 * EDGE, NY + 16, NZ), jnp.float32)]
    res_shape = jax.ShapeDtypeStruct((REC, NZ), jnp.float32)
    own_cost = dict(flops=ROWS * NY * NZ * 60, nbytes=8 * ROWS * NY * NZ * 4)
    edge_cost = dict(flops=EDGE * NY * NZ * 10, nbytes=6 * EDGE * NY * NZ * 4)
    ANY = pl.BlockSpec(memory_space=pl.ANY)
    source = (first, source_cell, wavelet)
    taken = (first, receiver_cells, lists)

    def edges(forward, tick, sent, bases, parts):
        outs = [None, None]
        done = bases[0]
        for high in (True, False):
            side = 2 if high else 0
            smem = source if forward else taken
            outs[high] = call(
                functools.partial(edge_kernel, forward, tick, high),
                [planes(EDGE)] * (2 if forward else 1),
                [],
                [SMEM] * 3 + [VMEM] * 4 + [ANY],
                [VMEM] * (2 if forward else 1),
                name="edge_high" if high else "edge_low",
                **edge_cost,
            )(*smem, sent[high], bases[high], model[side], parts[high], done)
            done = outs[high][0]
        return outs

    def halos(cur, tick):
        low = swap(cur[0], "dom", starts)
        high = swap(cur[2], "dom", ends)
        return low, high

    old, cur = cut(wave_prev[0]), cut(wave_now[0])
    images, residuals = [], []
    for tick in range(STEPS):
        sent = halos(cur, tick)
        extra = (observed,) if tick > 0 else ()
        smem = ((first, receiver_cells, lists) if tick > 0 else (first,)) + (source_cell, wavelet) + extra
        outs = [planes(MID), planes(EDGE), planes(EDGE), planes(EDGE), planes(MID), planes(EDGE)]
        outs += [res_shape] if tick > 0 else []
        result = call(
            functools.partial(own_kernel, True, tick, False),
            outs,
            pad,
            [SMEM] * len(smem) + [VMEM] * 9,
            [VMEM] * len(outs),
            name="own_forward",
            **own_cost,
        )(*smem, *cur, *old, *model)
        mid, base_lo, base_hi, part_lo, image_mid, part_hi = result[:6]
        if tick > 0:
            residuals.append(result[6])
        (low, image_lo), (high, image_hi) = edges(True, tick, sent, (base_lo, base_hi), (part_lo, part_hi))
        images.append((image_lo, image_mid, image_hi))
        old, cur = cur, (low, mid, high)
    last = cur
    old, cur = cut(adjoint_next[0]), cut(adjoint_now[0])
    grad = None
    for tick in reversed(range(STEPS)):
        sent = halos(cur, tick)
        top = tick == STEPS - 1
        extra = (observed,) if top else ()
        fields = last if top else (residuals[tick], *images[tick + 1], grad)
        outs = [planes(MID), planes(EDGE), planes(EDGE)]
        outs += [res_shape] if top else []
        outs += [planes(ROWS)]
        result = call(
            functools.partial(own_kernel, False, tick, not top),
            outs,
            pad,
            [SMEM] * (3 + len(extra)) + [VMEM] * (9 + len(fields)),
            [VMEM] * len(outs),
            name="own_adjoint",
            **own_cost,
        )(*taken, *extra, *cur, *old, *model, *fields)
        mid, base_lo, base_hi = result[:3]
        if top:
            residuals.append(result[3])
        grad = result[-1]
        (low,), (high,) = edges(False, tick, sent, (base_lo, base_hi), (residuals[tick],) * 2)
        old, cur = cur, (low, mid, high)
    grad = call(
        join_kernel,
        planes(ROWS),
        [],
        [SMEM] + [VMEM] * 7,
        VMEM,
        2 * ROWS * NY * NZ,
        4 * ROWS * NY * NZ * 4,
        "join",
    )(first, grad, *cur, *images[0])
    total = shot_sum(grad)
    peak = dom_max(jnp.max(jnp.abs(total)))
    direction = total / (peak + EPSILON)
    new_model = model_slab * (1.0 - STEP_FRACTION * direction)
    return direction, new_model


def solution(mesh):
    placed = (
        P("dom", None, None),
        P("shot", "dom", None, None),
        P("shot", "dom", None, None),
        P("shot", "dom", None, None),
        P("shot", "dom", None, None),
        P("shot", None),
        P("shot"),
        P("shot", None),
        P("shot", None, None),
    )
    return jax.shard_map(
        on_device,
        mesh=mesh,
        in_specs=placed,
        out_specs=(P("dom", None, None), P("dom", None, None)),
        check_vma=False,
    )
```
